32 devices in a mesh: dp: 8 (over y, x, core), mp: 4 (over z).
Axes of the slice: x: 2, y: 2, z: 4, core: 2. Of those that a mesh axis runs over, the one named last changes fastest.
Arguments:
- features: bfloat16 [4, 4096, 1152], P('mp', 'dp'), may hold values from -6 to 6
- context_gain: float32 [1152], replicated, may hold values from 0.1 to 1.9
- queries: bfloat16 [64, 1536], replicated, may hold values from -136 to 136
- w_key: bfloat16 [1152, 384], replicated, may hold values from -0.1875 to 0.1875
- w_value: bfloat16 [1152, 384], replicated, may hold values from -0.1875 to 0.1875
- w_out: bfloat16 [1536, 2048], replicated, may hold values from -0.15625 to 0.15625
- image_tiles: int32 [4, 2], P('mp'), may hold values from 1024 to 3072, as said below
- slot_start: int32 [4, 2], P('mp'), may hold values from 0 to 64
- text_rows: bfloat16 [4, 1024, 2048], P('mp', 'dp'), may hold values from -6 to 6
- row_grads: bfloat16 [4, 1024, 2048], P('mp', 'dp'), may hold values from -6 to 6
Outputs:
- merged_rows: bfloat16 [4, 1024, 2048], P('mp', 'dp')
- query_grad: float32 [64, 1536], replicated
The draws below stay inside these ranges and needn't reach their ends.
Inputs may be any that keep to these rules, and one draw needn't show every extreme that they name: `image_tiles`: the 2 images of a group fill its 4096 rows in order; every image takes 2 * 512 to 3072 rows, and in every group one image takes exactly 1024 and one exactly 3072.
All inputs are finite; a program needn't handle non-finite values.
Results may differ from the reference program's by a relative error of at most 0.005.
The reference program's roundings to bfloat16 on the way (of `normed`, `key_rows`, `projected`, `upstream` and `score_grad`) count: a program that leaves them out, or rounds other values in their place, can miss the bound.
Values may be sent and summed in bfloat16 or wider, within the bound.
A program may use at most 128 MiB of HBM per device.

```python
import jax
import jax.numpy as jnp
from jax import lax

VW = 1152
HEADS = 16
HEAD = 96
KVH = 4
LAT = 64
DM = 2048
TOK_DEV = 512
SEQ_DEV = 128
IMAGES = 2
ROWS = 4096
GROUPS = 4
SEQ_ROWS = 1024
N_DP = 8
N_MP = 4


def draw_queries(key, part):
    base_values = 2.0 * jax.random.normal(key, (LAT, HEADS * HEAD), jnp.float32)
    return jnp.clip(base_values, -12.0, 12.0).astype(jnp.bfloat16)


def segment_sizes(key, count):
    pair_count = count // 2
    shifts = jax.random.randint(key, (N_MP, pair_count), 0, 2 * TOK_DEV + 1).astype(jnp.int32)
    shifts = shifts.at[:, 0].set(2 * TOK_DEV)
    sizes = jnp.concatenate([4 * TOK_DEV + shifts, 4 * TOK_DEV - shifts], axis=1).astype(jnp.int32)
    if count % 2 == 1:
        sizes = jnp.concatenate([sizes, jnp.full((N_MP, 1), 4 * TOK_DEV, jnp.int32)], axis=1)
    return sizes


def draw_image_tiles(key, part):
    if N_DP >= 16:
        count = IMAGES // 2
        pair_count = count // 2
        lower = segment_sizes(jax.random.fold_in(key, 21), count)
        lower = lower.at[:, pair_count].add(TOK_DEV // 2)
        upper = segment_sizes(jax.random.fold_in(key, 23), IMAGES - count)
        upper = upper.at[:, 0].add(-(TOK_DEV // 2))
        lower = jax.random.permutation(jax.random.fold_in(key, 25), lower, axis=1, independent=True)
        upper = jax.random.permutation(jax.random.fold_in(key, 27), upper, axis=1, independent=True)
        return jnp.concatenate([lower, upper], axis=1).astype(jnp.int32)
    pair_count = IMAGES // 2
    cut_key = jax.random.fold_in(key, 11)
    order_key = jax.random.fold_in(key, 13)
    shifts = jax.random.randint(cut_key, (N_MP, pair_count), 0, 2 * TOK_DEV + 1).astype(jnp.int32)
    shifts = shifts.at[:, 0].set(2 * TOK_DEV)
    extra_rows = jnp.concatenate([2 * TOK_DEV + shifts, 2 * TOK_DEV - shifts], axis=1).astype(jnp.int32)
    extra_rows = jax.random.permutation(order_key, extra_rows, axis=1, independent=True)
    return (2 * TOK_DEV + extra_rows).astype(jnp.int32)


def plant(result, rng, smallest, top_value):
    extent = result.shape
    place = [jax.random.randint(jax.random.fold_in(rng, axis), (), 0, extent[axis]) for axis in range(len(extent))]
    result = result.at[tuple(place)].set(smallest)
    longest = extent.index(max(extent))
    place[longest] = (place[longest] + 1) % extent[longest]
    return result.at[tuple(place)].set(top_value)


def block_levels(key, shape, cuts, smallest, top_value):
    level = 1.0
    for axis_at, blocks in cuts:
        draws = jax.random.uniform(jax.random.fold_in(jax.random.fold_in(key, 6), axis_at), (blocks,), jnp.float32, smallest / len(cuts), top_value / len(cuts))
        level = level * jnp.repeat(jnp.exp(draws), shape[axis_at] // blocks).reshape((-1,) + (1,) * (len(shape) - 1 - axis_at))
    return level


def noise(own_key, dims, scale, reach, shards=(), kind=jnp.bfloat16):
    level = block_levels(own_key, dims, shards, -0.22, 0.18) if shards else 1.0
    values = jax.random.normal(own_key, dims, jnp.float32) * scale * level
    return jnp.minimum(jnp.maximum(values, -reach), reach).astype(kind)


def setup_inputs(seed: int = 0) -> dict:
    key_of = jax.random.split(jax.random.key(seed), 11)
    features = noise(key_of[0], (GROUPS, ROWS, VW), 1.0, 6.0, ((0, 4), (1, 8)))
    context_gain = jnp.clip(1.0 + 0.18 * jax.random.normal(key_of[1], (VW,), jnp.float32), 0.1, 1.9)
    queries = draw_queries(jax.random.fold_in(key_of[10], 71), 0)
    w_key = noise(key_of[3], (VW, KVH * HEAD), VW ** -0.5, 0.1875)
    w_value = noise(key_of[4], (VW, KVH * HEAD), VW ** -0.5, 0.1875)
    w_out = noise(key_of[5], (HEADS * HEAD, DM), (HEADS * HEAD) ** -0.5, 0.15625)
    image_tiles = draw_image_tiles(jax.random.fold_in(key_of[10], 71), 0)
    slot_start = plant(jax.random.randint(key_of[7], (GROUPS, IMAGES), 0, SEQ_DEV - LAT + 1), jax.random.fold_in(key_of[7], 1), 0, SEQ_DEV - LAT).astype(jnp.int32)
    text_rows = noise(key_of[8], (GROUPS, SEQ_ROWS, DM), 1.0, 6.0, ((0, 4), (1, 8)))
    row_grads = noise(key_of[9], (GROUPS, SEQ_ROWS, DM), 1.0, 6.0, ((0, 4), (1, 8)))
    return dict(features=features, context_gain=context_gain, queries=queries, w_key=w_key, w_value=w_value, w_out=w_out, image_tiles=image_tiles, slot_start=slot_start, text_rows=text_rows, row_grads=row_grads)


epsilon = 1e-06

def normalize(features, context_gain):
    widened = features.astype(jnp.float32)
    mean_square = lax.optimization_barrier(jnp.mean(widened * widened, axis=-1, keepdims=True))
    return (widened * lax.rsqrt(mean_square + epsilon) * context_gain).astype(jnp.bfloat16)

def group_pass(queries, w_key, w_value, w_out, context_gain, group_data):
    features, tiles, slots, text, grads = group_data
    rows_all = features.shape[0]
    group_heads = HEADS // KVH
    scale = HEAD ** (-0.5)
    normed = normalize(features, context_gain)
    key_rows = jnp.dot(normed, w_key, preferred_element_type=jnp.float32).astype(jnp.bfloat16)
    value_rows = jnp.dot(normed, w_value, preferred_element_type=jnp.float32).astype(jnp.bfloat16)
    key_heads = key_rows.astype(jnp.float32).reshape(rows_all, KVH, HEAD)
    value_heads = value_rows.astype(jnp.float32).reshape(rows_all, KVH, HEAD)
    query_heads = queries.astype(jnp.float32).reshape(LAT, KVH, group_heads, HEAD)
    scores = jnp.einsum('lgce,rge->gclr', query_heads, key_heads) * scale
    image_ends = jnp.cumsum(tiles).astype(jnp.int32)
    positions = jnp.arange(rows_all, dtype=jnp.int32)
    image_of = lax.optimization_barrier(jnp.sum((positions[:, None] >= image_ends[None, :]).astype(jnp.int32), axis=1)).astype(jnp.int32)
    flat_scores = scores.reshape(-1, rows_all).T
    image_peak = jax.ops.segment_max(flat_scores, image_of, num_segments=IMAGES)
    weights = jnp.exp(flat_scores - image_peak[image_of])
    image_total = jax.ops.segment_sum(weights, image_of, num_segments=IMAGES)
    rounded = weights.astype(jnp.bfloat16).astype(jnp.float32)
    block_count = rows_all // TOK_DEV
    rounded_blocks = rounded.reshape(block_count, TOK_DEV, KVH, group_heads, LAT)
    value_blocks = value_heads.reshape(block_count, TOK_DEV, KVH, HEAD)
    key_blocks = key_heads.reshape(block_count, TOK_DEV, KVH, HEAD)
    image_blocks = image_of.reshape(block_count, TOK_DEV)
    image_ids = jnp.arange(IMAGES, dtype=jnp.int32)

    def accumulate(running, block):
        weight_blk, value_blk, image_blk = block
        first_image = image_blk[0]
        last_image = image_blk[-1]
        in_first = (image_blk == first_image).astype(jnp.float32)
        in_last = ((image_blk == last_image) & (last_image != first_image)).astype(jnp.float32)
        part_first = jnp.einsum('tgcl,tge->gcle', weight_blk * in_first[:, None, None, None], value_blk)
        part_last = jnp.einsum('tgcl,tge->gcle', weight_blk * in_last[:, None, None, None], value_blk)
        pick_first = (image_ids == first_image).astype(jnp.float32)[:, None, None, None, None]
        pick_last = (image_ids == last_image).astype(jnp.float32)[:, None, None, None, None]
        return (running + pick_first * part_first[None] + pick_last * part_last[None], None)
    start = jnp.zeros((IMAGES, KVH, group_heads, LAT, HEAD), jnp.float32)
    weighted, _ = lax.scan(accumulate, start, (rounded_blocks, value_blocks, image_blocks))
    totals = image_total.reshape(IMAGES, KVH, group_heads, LAT)
    attended = weighted / totals[..., None]
    attended_rows = attended.transpose(0, 3, 1, 2, 4).reshape(IMAGES, LAT, HEADS * HEAD)
    end_rows = ((image_ends - 1) // TOK_DEV * SEQ_DEV + slots).astype(jnp.int32)

    def place_rows(image_index, merged):
        projected = jnp.dot(attended_rows[image_index].astype(jnp.bfloat16), w_out, preferred_element_type=jnp.float32).astype(jnp.bfloat16)
        return lax.dynamic_update_slice(merged, projected, (end_rows[image_index], jnp.int32(0)))
    merged = lax.fori_loop(0, IMAGES, place_rows, text)

    def take_rows(image_index):
        taken = lax.dynamic_slice(grads, (end_rows[image_index], jnp.int32(0)), (LAT, DM))
        return jnp.dot(taken, w_out.T, preferred_element_type=jnp.float32).astype(jnp.bfloat16)
    upstream = jax.vmap(take_rows)(image_ids)
    grad_heads = upstream.astype(jnp.float32).reshape(IMAGES, LAT, KVH, group_heads, HEAD).transpose(0, 2, 3, 1, 4)
    inner = lax.optimization_barrier(jnp.sum(grad_heads * attended, axis=-1))
    probability = weights / image_total[image_of]
    inner_rows = inner.reshape(IMAGES, -1)[image_of]
    prob_blocks = probability.reshape(block_count, TOK_DEV, KVH, group_heads, LAT)
    inner_blocks = inner_rows.reshape(block_count, TOK_DEV, KVH, group_heads, LAT)

    def backward(running, block):
        prob_blk, inner_blk, value_blk, key_blk, image_blk = block
        first_image = image_blk[0]
        last_image = image_blk[-1]
        dot_first = jnp.einsum('gcle,tge->tgcl', grad_heads[first_image], value_blk)
        dot_last = jnp.einsum('gcle,tge->tgcl', grad_heads[last_image], value_blk)
        chosen = jnp.where((image_blk == first_image)[:, None, None, None], dot_first, dot_last)
        score_grad = (prob_blk * (chosen - inner_blk)).astype(jnp.bfloat16).astype(jnp.float32)
        return (running + jnp.einsum('tgcl,tge->lgce', score_grad, key_blk), None)
    start_grad = jnp.zeros((LAT, KVH, group_heads, HEAD), jnp.float32)
    grad_sum, _ = lax.scan(backward, start_grad, (prob_blocks, inner_blocks, value_blocks, key_blocks, image_blocks))
    return (merged, grad_sum.reshape(LAT, HEADS * HEAD) * scale)

def reference(features, context_gain, queries, w_key, w_value, w_out, image_tiles, slot_start, text_rows, row_grads):

    def one_group(group_data):
        return group_pass(queries, w_key, w_value, w_out, context_gain, group_data)
    merged, grads = lax.map(one_group, (features, image_tiles, slot_start, text_rows, row_grads))
    return (merged, lax.optimization_barrier(jnp.sum(grads, axis=0)))
```

```python
import functools

import jax
import jax.numpy as jnp
from jax import lax
from jax.experimental import pallas as pl
from jax.experimental.pallas import tpu as pltpu
from jax.sharding import PartitionSpec as P

HEADS = 16
HEAD = 96
KVH = 4
PER = HEADS // KVH
epsilon = 1e-06
LOW = -1e30
MESH = pl.DeviceIdType.MESH
F32 = jnp.float32
BF16 = jnp.bfloat16


def to_cols(rows):
    stacked = jnp.concatenate([rows[:, c * HEAD : (c + 1) * HEAD] for c in range(PER)], axis=0)
    return stacked.T


def to_rows(cols, lat):
    flipped = cols.T
    return jnp.concatenate(
        [
            flipped[c * lat : (c + 1) * lat, g * HEAD : (g + 1) * HEAD]
            for g in range(KVH)
            for c in range(PER)
        ],
        axis=1,
    )


def dot(a, b):
    return jnp.dot(a, b, preferred_element_type=F32)


class Gather:
    def __init__(self, chips, chip, core, at, send, recv):
        self.chips, self.chip, self.core = chips, chip, core
        self.at, self.send, self.recv = at, send, recv

    def hop(self, slot_chip, sem, target):
        ref = self.at(slot_chip, self.core)
        return pltpu.make_async_remote_copy(
            src_ref=ref,
            dst_ref=ref,
            send_sem=self.send.at[sem],
            recv_sem=self.recv.at[sem],
            device_id={"dp": target},
            device_id_type=MESH,
        )

    def start(self):
        for k in range(1, self.chips):
            there = lax.rem(self.chip + k, self.chips)
            self.hop(self.chip, k, there * 2 + self.core).start()
        self.hop(self.chip, 0, self.chip * 2 + 1 - self.core).start()

    def forward(self):
        for k in range(1, self.chips):
            origin = lax.rem(self.chip + self.chips - k, self.chips)
            self.hop(origin, k, origin * 2 + self.core).wait_recv()
            self.hop(origin, self.chips - 1 + k, self.chip * 2 + 1 - self.core).start()

    def finish(self):
        mate = self.chip * 2 + 1 - self.core
        for k in range(self.chips):
            origin = lax.rem(self.chip + self.chips - k, self.chips)
            ref = self.at(origin, 1 - self.core)
            sem = 0 if k == 0 else self.chips - 1 + k
            pltpu.make_async_remote_copy(
                src_ref=ref,
                dst_ref=ref,
                send_sem=self.send.at[sem],
                recv_sem=self.recv.at[sem],
                device_id={"dp": mate},
                device_id_type=MESH,
            ).wait_recv()
        for sem in range(2 * self.chips - 1):
            self.hop(self.chip, sem, mate).wait_send()


def kernel(
    dims,
    tiles,
    slots,
    gain,
    queries,
    features_hbm,
    wk_hbm,
    wv_hbm,
    wo_hbm,
    text_hbm,
    grads_hbm,
    merged,
    query_grad,
    features,
    wk,
    wv,
    wo,
    text,
    grads,
    keys,
    values,
    keys_t,
    values_t,
    query_t,
    weights,
    chosen,
    sums,
    u_own,
    u_recv,
    u_all,
    stats,
    g_own,
    g_recv,
    g_pair,
    g_chip,
    z_all,
    g_all,
    a_own,
    a_recv,
    a_pair,
    a_chip,
    a_all,
    load_sem,
    pair_send,
    pair_recv,
    u_send,
    u_got,
    s_send,
    s_got,
    gc_send,
    gc_got,
    z_send,
    z_got,
    g_send,
    g_got,
    ac_send,
    ac_got,
    a_send,
    a_got,
):
    n_dp, n_mp, images, lat, tok, seq = dims
    chips = n_dp // 2
    me = lax.axis_index("dp")
    z = lax.axis_index("mp")
    chip = lax.div(me, 2)
    core = lax.rem(me, 2)
    mate = chip * 2 + 1 - core
    scale = HEAD ** (-0.5)
    half = KVH * HEAD // 2
    block = KVH * HEAD

    loads = []

    def load(src, dst, at):
        copy = pltpu.make_async_copy(src, dst, load_sem.at[at])
        copy.start()
        return copy

    features_in = load(features_hbm, features, 0)
    grads_in = load(grads_hbm, grads, 1)
    wo_in = [
        load(wo_hbm.at[pl.ds(g * block, block)], wo.at[pl.ds(g * block, block)], 2 + g)
        for g in range(KVH)
    ]
    wk_in = load(wk_hbm, wk, 2 + KVH)
    wv_in = load(wv_hbm, wv, 3 + KVH)
    text_in = load(text_hbm, text, 4 + KVH)

    barrier = pltpu.get_barrier_semaphore()
    pl.semaphore_signal(barrier, inc=1, device_id={"dp": mate}, device_id_type=MESH)
    for k in range(1, chips):
        pl.semaphore_signal(
            barrier,
            inc=1,
            device_id={"dp": lax.rem(chip + k, chips) * 2 + core},
            device_id_type=MESH,
        )
    for k in range(1, n_mp):
        pl.semaphore_signal(
            barrier, inc=1, device_id={"mp": lax.rem(z + k, n_mp)}, device_id_type=MESH
        )

    def pair_copy(src, dst, at):
        return pltpu.make_async_remote_copy(
            src_ref=src,
            dst_ref=dst,
            send_sem=pair_send.at[at],
            recv_sem=pair_recv.at[at],
            device_id={"dp": mate},
            device_id_type=MESH,
        )

    first_row = me * tok
    ends = []
    running = jnp.int32(0)
    for i in range(images):
        running = running + tiles[0, i]
        ends.append(running)

    def image_at(row):
        found = jnp.int32(0)
        for end in ends:
            found = found + jnp.where(row >= end, 1, 0)
        return found

    def pick(options, index):
        chosen_one = options[0]
        for i in range(1, images):
            chosen_one = jnp.where(index == i, options[i], chosen_one)
        return chosen_one

    first = image_at(first_row)
    last = image_at(first_row + tok - 1)
    end_first = pick(ends, first)
    end_last = pick(ends, last)
    ends_here = end_first <= first_row + tok
    slot = pick([slots[0, i] for i in range(images)], first)
    slot = jnp.where(ends_here, slot, 2 * seq)
    rows_at = first_row + lax.broadcasted_iota(jnp.int32, (tok, 1), 0)
    in_first = rows_at < end_first

    features_in.wait()
    wide = features[0].astype(F32)
    mean_square = jnp.mean(wide * wide, axis=-1, keepdims=True)
    features[0] = (wide * lax.rsqrt(mean_square + epsilon) * gain[...]).astype(BF16)

    grads_in.wait()
    take = (
        lax.broadcasted_iota(jnp.int32, (lat, seq), 0) + slot
        == lax.broadcasted_iota(jnp.int32, (lat, seq), 1)
    )
    taken = dot(jnp.where(take, 1.0, 0.0).astype(BF16), grads[0]).astype(BF16)
    for g in range(KVH):
        wo_in[g].wait()
        up = lax.dot_general(
            taken,
            wo[g * block : (g + 1) * block, :],
            (((1,), (1,)), ((), ())),
            preferred_element_type=F32,
        )
        u_own[(g * HEAD) // half, pl.ds((g * HEAD) % half, HEAD), :] = to_cols(up).astype(BF16)
    pl.semaphore_wait(barrier, chips + n_mp - 1)
    u_pair = pair_copy(u_own.at[1 - core], u_recv, 0)
    u_pair.start()

    wk_in.wait()
    projected_keys = dot(features[0], wk[...])
    keys_t[...] = projected_keys.T.astype(BF16)
    for g in range(KVH):
        keys[g] = projected_keys[:, g * HEAD : (g + 1) * HEAD].astype(BF16)
    u_gather = Gather(chips, chip, core, lambda j, c: u_all.at[j, c], u_send, u_got)
    u_pair.wait()
    u_all[chip, core] = u_own[core] + u_recv[...]
    u_gather.start()
    wv_in.wait()
    projected_values = dot(features[0], wv[...])
    values_t[...] = projected_values.T.astype(BF16)
    for g in range(KVH):
        values[g] = projected_values[:, g * HEAD : (g + 1) * HEAD].astype(BF16)
    for g in range(KVH):
        query_t[g] = to_cols(queries[:, g * block : (g + 1) * block].astype(F32)).astype(BF16)

    peaks, totals = ([[], []], [[], []])
    for g in range(KVH):
        scores = dot(keys[g], query_t[g]) * scale
        peak_first = jnp.max(jnp.where(in_first, scores, LOW), axis=0, keepdims=True)
        peak_last = jnp.max(jnp.where(in_first, LOW, scores), axis=0, keepdims=True)
        weight = jnp.exp(scores - jnp.where(in_first, peak_first, peak_last))
        weights[g] = weight
        weight_first = jnp.where(in_first, weight, 0.0)
        weight_last = jnp.where(in_first, 0.0, weight)
        peaks[0].append(peak_first)
        peaks[1].append(peak_last)
        totals[0].append(jnp.sum(weight_first, axis=0, keepdims=True))
        totals[1].append(jnp.sum(weight_last, axis=0, keepdims=True))
        value_cols = values_t[pl.ds(g * HEAD, HEAD), :]
        sums[0, g] = dot(value_cols, weight_first.astype(BF16))
        sums[1, g] = dot(value_cols, weight_last.astype(BF16))
        if g == KVH - 2:
            u_gather.forward()
    u_gather.finish()

    chip_first = lax.div(end_first - 1, 2 * tok)
    chip_last = lax.div(end_last - 1, 2 * tok)

    def up_of(where_from, g):
        at = g * HEAD
        return u_all[where_from, at // half, pl.ds(at % half, HEAD), :]

    dots = [
        [
            jnp.sum(up_of(where_from, g).astype(F32) * sums[part, g], axis=0, keepdims=True)
            for g in range(KVH)
        ]
        for part, where_from in enumerate((chip_first, chip_last))
    ]
    stats[chip, core] = jnp.concatenate(
        peaks[0] + totals[0] + dots[0] + peaks[1] + totals[1] + dots[1], axis=0
    )
    s_gather = Gather(chips, chip, core, lambda j, c: stats.at[j, c], s_send, s_got)
    s_gather.start()
    for g in range(KVH):
        dot_first = dot(values[g], up_of(chip_first, g))
        dot_last = dot(values[g], up_of(chip_last, g))
        chosen[g] = jnp.where(in_first, dot_first, dot_last)
        if g == KVH // 2 - 1:
            s_gather.forward()
    s_gather.finish()

    own = stats[chip, core]
    parts = []
    for d in range(n_dp):
        got = stats[d // 2, d % 2]
        for part, image in enumerate((image_at(d * tok), image_at(d * tok + tok - 1))):
            at = 3 * KVH * part
            parts.append(
                (image, got[at : at + KVH], got[at + KVH : at + 2 * KVH], got[at + 2 * KVH : at + 3 * KVH])
            )

    def whole(mine, local_peak):
        peak = jnp.full_like(local_peak, LOW)
        for image, part_peak, _, _ in parts:
            peak = jnp.maximum(peak, jnp.where(image == mine, part_peak, LOW))
        total = jnp.zeros_like(peak)
        inner = jnp.zeros_like(peak)
        for image, part_peak, part_total, part_dot in parts:
            factor = jnp.where(image == mine, jnp.exp(part_peak - peak), 0.0)
            total = total + jnp.where(image == mine, part_total * factor, 0.0)
            inner = inner + jnp.where(image == mine, part_dot * factor, 0.0)
        return jnp.exp(local_peak - peak) / total, inner / total

    factor_first, inner_first = whole(first, own[0:KVH])
    factor_last, inner_last = whole(last, own[3 * KVH : 4 * KVH])

    for g in range(KVH):
        prob = weights[g] * jnp.where(
            in_first, factor_first[g : g + 1], factor_last[g : g + 1]
        )
        grad = prob * (
            chosen[g] - jnp.where(in_first, inner_first[g : g + 1], inner_last[g : g + 1])
        )
        term = dot(keys_t[pl.ds(g * HEAD, HEAD), :], grad.astype(BF16)) * scale
        lanes = term.shape[1] // 2
        for part in range(2):
            g_own[part, pl.ds(g * HEAD, HEAD), :] = term[:, part * lanes : (part + 1) * lanes]
    g_pair_copy = pair_copy(g_own.at[1 - core], g_recv, 1)
    g_pair_copy.start()

    for g in range(KVH):
        share_first = sums[0, g] * factor_first[g : g + 1]
        share_last = sums[1, g] * factor_last[g : g + 1]
        for i in range(images):
            share = jnp.where(first == i, share_first, 0.0) + jnp.where(last == i, share_last, 0.0)
            at = g * HEAD
            a_own[at // half, pl.ds(i * half + at % half, HEAD), :] = share.astype(BF16)
    a_pair_copy = pair_copy(a_own.at[1 - core], a_recv, 2)
    a_pair_copy.start()

    def scatter(src, rows, dst, send, recv, k, target_chip):
        return pltpu.make_async_remote_copy(
            src_ref=src.at[pl.ds(pl.multiple_of(target_chip * rows, rows), rows)],
            dst_ref=dst.at[k],
            send_sem=send.at[k],
            recv_sem=recv.at[k],
            device_id={"dp": target_chip * 2 + core},
            device_id_type=MESH,
        )

    g_rows = g_pair.shape[0] // chips
    a_rows = a_pair.shape[0] // chips
    g_pair_copy.wait()
    g_pair[...] = g_own[core] + g_recv[...]
    g_scatter = [
        scatter(g_pair, g_rows, g_chip, gc_send, gc_got, k, lax.rem(chip + k, chips))
        for k in range(1, chips)
    ]
    for copy in g_scatter:
        copy.start()
    a_pair_copy.wait()
    a_pair[...] = (a_own[core].astype(F32) + a_recv[...].astype(F32)).astype(BF16)
    a_scatter = [
        scatter(a_pair, a_rows, a_chip, ac_send, ac_got, k, lax.rem(chip + k, chips))
        for k in range(1, chips)
    ]
    for copy in a_scatter:
        copy.start()

    for copy in g_scatter:
        copy.wait()
    g_piece = g_pair[pl.ds(pl.multiple_of(chip * g_rows, g_rows), g_rows), :]
    for k in range(1, chips):
        g_piece = g_piece + g_chip[k]
    z_all[z] = g_piece
    z_copies = [
        pltpu.make_async_remote_copy(
            src_ref=z_all.at[z],
            dst_ref=z_all.at[z],
            send_sem=z_send.at[k],
            recv_sem=z_got.at[k],
            device_id={"mp": lax.rem(z + k, n_mp)},
            device_id_type=MESH,
        )
        for k in range(1, n_mp)
    ]
    for copy in z_copies:
        copy.start()

    for copy in a_scatter:
        copy.wait()
    a_piece = a_pair[pl.ds(pl.multiple_of(chip * a_rows, a_rows), a_rows), :].astype(F32)
    for k in range(1, chips):
        a_piece = a_piece + a_chip[k].astype(F32)
    a_all[core, pl.ds(pl.multiple_of(chip * a_rows, a_rows), a_rows), :] = a_piece.astype(BF16)
    a_gather = Gather(
        chips,
        chip,
        core,
        lambda j, c: a_all.at[c, pl.ds(pl.multiple_of(j * a_rows, a_rows), a_rows)],
        a_send,
        a_got,
    )
    a_gather.start()

    for k in range(1, n_mp):
        origin = lax.rem(z + n_mp - k, n_mp)
        pltpu.make_async_remote_copy(
            src_ref=z_all.at[origin],
            dst_ref=z_all.at[origin],
            send_sem=z_send.at[k],
            recv_sem=z_got.at[k],
            device_id={"mp": origin},
            device_id_type=MESH,
        ).wait_recv()
    g_sum = z_all[0]
    for k in range(1, n_mp):
        g_sum = g_sum + z_all[k]
    g_all[core, pl.ds(pl.multiple_of(chip * g_rows, g_rows), g_rows), :] = g_sum
    g_gather = Gather(
        chips,
        chip,
        core,
        lambda j, c: g_all.at[c, pl.ds(pl.multiple_of(j * g_rows, g_rows), g_rows)],
        g_send,
        g_got,
    )
    g_gather.start()
    for copy in z_copies:
        copy.wait_send()

    a_gather.forward()
    g_gather.forward()
    a_gather.finish()
    halves = []
    for part in range(2):
        attended = a_all[part, 0:half, :].astype(F32)
        for i in range(1, images):
            other = a_all[part, i * half : (i + 1) * half, :].astype(F32)
            attended = jnp.where(first == i, other, attended)
        halves.append(attended)
    attended_rows = to_rows(jnp.concatenate(halves, axis=0), lat).astype(BF16)
    put = (
        lax.broadcasted_iota(jnp.int32, (seq, lat), 1) + slot
        == lax.broadcasted_iota(jnp.int32, (seq, lat), 0)
    )
    shifted = dot(jnp.where(put, 1.0, 0.0).astype(BF16), attended_rows).astype(BF16)
    row_at = lax.broadcasted_iota(jnp.int32, (seq, 1), 0)
    inside = (row_at >= slot) & (row_at < slot + lat)
    text_in.wait()
    projected = dot(shifted, wo[...]).astype(BF16)
    merged[0] = jnp.where(inside, projected.astype(F32), text[0].astype(F32)).astype(BF16)

    g_gather.finish()
    query_grad[...] = to_rows(jnp.concatenate([g_all[0], g_all[1]], axis=1), lat)


def on_device(
    n_dp, n_mp, features, context_gain, queries, w_key, w_value, w_out, image_tiles, slot_start, text_rows, row_grads
):
    _, tok, width = features.shape
    images = image_tiles.shape[1]
    lat = queries.shape[0]
    _, seq, dm = text_rows.shape
    chips = n_dp // 2
    block = KVH * HEAD
    half = block // 2
    cols = PER * lat
    a_rows = images * half // chips
    g_rows = block // chips
    gathers = pltpu.SemaphoreType.DMA((2 * chips - 1,))
    vmem = pl.BlockSpec(memory_space=pltpu.VMEM)
    smem = pl.BlockSpec(memory_space=pltpu.SMEM)
    anywhere = pl.BlockSpec(memory_space=pl.ANY)
    return pl.pallas_call(
        functools.partial(kernel, (n_dp, n_mp, images, lat, tok, seq)),
        out_shape=(
            jax.ShapeDtypeStruct(text_rows.shape, BF16),
            jax.ShapeDtypeStruct(queries.shape, F32),
        ),
        in_specs=[smem, smem, vmem, vmem] + [anywhere] * 6,
        out_specs=(vmem, vmem),
        scratch_shapes=[
            pltpu.VMEM(features.shape, BF16),
            pltpu.VMEM(w_key.shape, BF16),
            pltpu.VMEM(w_value.shape, BF16),
            pltpu.VMEM(w_out.shape, BF16),
            pltpu.VMEM(text_rows.shape, BF16),
            pltpu.VMEM(row_grads.shape, BF16),
            pltpu.VMEM((KVH, tok, HEAD), BF16),
            pltpu.VMEM((KVH, tok, HEAD), BF16),
            pltpu.VMEM((block, tok), BF16),
            pltpu.VMEM((block, tok), BF16),
            pltpu.VMEM((KVH, HEAD, cols), BF16),
            pltpu.VMEM((KVH, tok, cols), F32),
            pltpu.VMEM((KVH, tok, cols), F32),
            pltpu.VMEM((2, KVH, HEAD, cols), F32),
            pltpu.VMEM((2, half, cols), BF16),
            pltpu.VMEM((half, cols), BF16),
            pltpu.VMEM((chips, 2, half, cols), BF16),
            pltpu.VMEM((chips, 2, 6 * KVH, cols), F32),
            pltpu.VMEM((2, block, cols // 2), F32),
            pltpu.VMEM((block, cols // 2), F32),
            pltpu.VMEM((block, cols // 2), F32),
            pltpu.VMEM((chips, g_rows, cols // 2), F32),
            pltpu.VMEM((n_mp, g_rows, cols // 2), F32),
            pltpu.VMEM((2, block, cols // 2), F32),
            pltpu.VMEM((2, images * half, cols), BF16),
            pltpu.VMEM((images * half, cols), BF16),
            pltpu.VMEM((images * half, cols), BF16),
            pltpu.VMEM((chips, a_rows, cols), BF16),
            pltpu.VMEM((2, images * half, cols), BF16),
            pltpu.SemaphoreType.DMA((5 + KVH,)),
            pltpu.SemaphoreType.DMA((3,)),
            pltpu.SemaphoreType.DMA((3,)),
            gathers,
            gathers,
            gathers,
            gathers,
            pltpu.SemaphoreType.DMA((chips,)),
            pltpu.SemaphoreType.DMA((chips,)),
            pltpu.SemaphoreType.DMA((n_mp,)),
            pltpu.SemaphoreType.DMA((n_mp,)),
            gathers,
            gathers,
            pltpu.SemaphoreType.DMA((chips,)),
            pltpu.SemaphoreType.DMA((chips,)),
            gathers,
            gathers,
        ],
        compiler_params=pltpu.CompilerParams(
            collective_id=0, has_side_effects=True, vmem_limit_bytes=60 * 1024 * 1024
        ),
        name="resampler",
    )(
        image_tiles,
        slot_start,
        context_gain.reshape(1, -1),
        queries,
        features,
        w_key,
        w_value,
        w_out,
        text_rows,
        row_grads,
    )


def solution(mesh):
    placed = (
        P("mp", "dp", None),
        P(),
        P(),
        P(),
        P(),
        P(),
        P("mp", None),
        P("mp", None),
        P("mp", "dp", None),
        P("mp", "dp", None),
    )
    return jax.shard_map(
        functools.partial(on_device, mesh.shape["dp"], mesh.shape["mp"]),
        mesh=mesh,
        in_specs=placed,
        out_specs=(P("mp", "dp", None), P()),
        check_vma=False,
    )
```

```python
import functools

import jax
import jax.numpy as jnp
from jax import lax
from jax.experimental import pallas as pl
from jax.experimental.pallas import tpu as pltpu
from jax.sharding import PartitionSpec as P

HEADS = 16
HEAD = 96
KVH = 4
PER = HEADS // KVH
epsilon = 1e-06
LOW = -1e30
MESH = pl.DeviceIdType.MESH
F32 = jnp.float32
BF16 = jnp.bfloat16


def to_cols(rows):
    stacked = jnp.concatenate([rows[:, c * HEAD : (c + 1) * HEAD] for c in range(PER)], axis=0)
    return stacked.T


def to_rows(cols, lat):
    flipped = cols.T
    return jnp.concatenate(
        [
            flipped[c * lat : (c + 1) * lat, g * HEAD : (g + 1) * HEAD]
            for g in range(KVH)
            for c in range(PER)
        ],
        axis=1,
    )


def dot(a, b):
    return jnp.dot(a, b, preferred_element_type=F32)


class Gather:
    def __init__(self, chips, chip, core, at, send, recv):
        self.chips, self.chip, self.core = chips, chip, core
        self.at, self.send, self.recv = at, send, recv

    def hop(self, slot_chip, sem, target):
        ref = self.at(slot_chip, self.core)
        return pltpu.make_async_remote_copy(
            src_ref=ref,
            dst_ref=ref,
            send_sem=self.send.at[sem],
            recv_sem=self.recv.at[sem],
            device_id={"dp": target},
            device_id_type=MESH,
        )

    def start(self):
        for k in range(1, self.chips):
            there = lax.rem(self.chip + k, self.chips)
            self.hop(self.chip, k, there * 2 + self.core).start()
        self.hop(self.chip, 0, self.chip * 2 + 1 - self.core).start()

    def forward(self):
        for k in range(1, self.chips):
            origin = lax.rem(self.chip + self.chips - k, self.chips)
            self.hop(origin, k, origin * 2 + self.core).wait_recv()
            self.hop(origin, self.chips - 1 + k, self.chip * 2 + 1 - self.core).start()

    def finish(self):
        mate = self.chip * 2 + 1 - self.core
        for k in range(self.chips):
            origin = lax.rem(self.chip + self.chips - k, self.chips)
            ref = self.at(origin, 1 - self.core)
            sem = 0 if k == 0 else self.chips - 1 + k
            pltpu.make_async_remote_copy(
                src_ref=ref,
                dst_ref=ref,
                send_sem=self.send.at[sem],
                recv_sem=self.recv.at[sem],
                device_id={"dp": mate},
                device_id_type=MESH,
            ).wait_recv()
        for sem in range(2 * self.chips - 1):
            self.hop(self.chip, sem, mate).wait_send()


class Direct:
    def __init__(self, chips, chip, core, src, dst, send, recv):
        self.chips, self.chip, self.core = chips, chip, core
        self.src, self.dst, self.send, self.recv = src, dst, send, recv

    def hop(self, k, q, origin, target):
        return pltpu.make_async_remote_copy(
            src_ref=self.src(*target),
            dst_ref=self.dst(*origin),
            send_sem=self.send.at[2 * k + q],
            recv_sem=self.recv.at[2 * k + q],
            device_id={"dp": target[0] * 2 + target[1]},
            device_id_type=MESH,
        )

    def other(self, k, q):
        return (lax.rem(self.chip + k, self.chips), 1 - self.core if q else self.core)

    def start(self, k, q):
        self.hop(k, q, (self.chip, self.core), self.other(k, q)).start()

    def all_start(self):
        for k in list(range(1, self.chips)) + [0]:
            for q in range(2):
                if k or q:
                    self.start(k, q)

    def finish(self):
        for k in range(self.chips):
            for q in range(2):
                if k or q:
                    origin = self.other(self.chips - k, q)
                    self.hop(k, q, origin, origin).wait_recv()
        for k in range(self.chips):
            for q in range(2):
                if k or q:
                    self.hop(k, q, (self.chip, self.core), self.other(k, q)).wait_send()


def kernel(
    dims,
    tiles,
    slots,
    gain,
    queries,
    features_hbm,
    wk_hbm,
    wv_hbm,
    wo_hbm,
    text_hbm,
    grads_hbm,
    merged,
    query_grad,
    features,
    wk,
    wv,
    wo,
    text,
    grads,
    keys,
    values,
    keys_t,
    values_t,
    query_t,
    weights,
    chosen,
    sums,
    u_own,
    u_recv,
    u_all,
    stats,
    dots,
    rescale,
    g_own,
    g_chip,
    z_all,
    g_all,
    a_own,
    a_recv,
    a_pair,
    a_chip,
    a_all,
    load_sem,
    pair_send,
    pair_recv,
    u_send,
    u_got,
    s_send,
    s_got,
    d_send,
    d_got,
    gc_send,
    gc_got,
    z_send,
    z_got,
    g_send,
    g_got,
    ac_send,
    ac_got,
    a_send,
    a_got,
):
    n_dp, n_mp, images, lat, tok, seq = dims
    chips = n_dp // 2
    me = lax.axis_index("dp")
    z = lax.axis_index("mp")
    chip = lax.div(me, 2)
    core = lax.rem(me, 2)
    mate = chip * 2 + 1 - core
    scale = HEAD ** (-0.5)
    half = KVH * HEAD // 2
    block = KVH * HEAD

    loads = []

    def load(src, dst, at):
        copy = pltpu.make_async_copy(src, dst, load_sem.at[at])
        copy.start()
        return copy

    def load_out(at, g):
        part = pl.ds(pl.multiple_of(g * block, block), block)
        return load(wo_hbm.at[part], wo.at[part], 2 + at)

    half_groups = KVH // 2
    order = [(1 - core) * half_groups + t for t in range(half_groups)]
    order += [core * half_groups + t for t in range(half_groups)]
    grads_in = load(grads_hbm, grads, 1)
    wo_in = [load_out(t, order[t]) for t in range(half_groups)]
    features_in = load(features_hbm, features, 0)
    wo_in += [load_out(t, order[t]) for t in range(half_groups, KVH)]
    wk_in = load(wk_hbm, wk, 2 + KVH)
    wv_in = load(wv_hbm, wv, 3 + KVH)
    text_in = load(text_hbm, text, 4 + KVH)

    barrier = pltpu.get_barrier_semaphore()
    for k in range(1, n_dp):
        pl.semaphore_signal(
            barrier, inc=1, device_id={"dp": lax.rem(me + k, n_dp)}, device_id_type=MESH
        )
    for k in range(1, n_mp):
        pl.semaphore_signal(
            barrier, inc=1, device_id={"mp": lax.rem(z + k, n_mp)}, device_id_type=MESH
        )

    def pair_copy(src, dst, at):
        return pltpu.make_async_remote_copy(
            src_ref=src,
            dst_ref=dst,
            send_sem=pair_send.at[at],
            recv_sem=pair_recv.at[at],
            device_id={"dp": mate},
            device_id_type=MESH,
        )

    first_row = me * tok
    ends = []
    running = jnp.int32(0)
    for i in range(images):
        running = running + tiles[0, i]
        ends.append(running)

    def image_at(row):
        found = jnp.int32(0)
        for end in ends:
            found = found + jnp.where(row >= end, 1, 0)
        return found

    def pick(options, index):
        chosen_one = options[0]
        for i in range(1, images):
            chosen_one = jnp.where(index == i, options[i], chosen_one)
        return chosen_one

    first = image_at(first_row)
    last = image_at(first_row + tok - 1)
    end_first = pick(ends, first)
    end_last = pick(ends, last)
    ends_here = end_first <= first_row + tok
    slot = pick([slots[0, i] for i in range(images)], first)
    slot = jnp.where(ends_here, slot, 2 * seq)
    rows_at = first_row + lax.broadcasted_iota(jnp.int32, (tok, 1), 0)
    in_first = rows_at < end_first

    for g in range(KVH):
        query_t[g] = to_cols(queries[:, g * block : (g + 1) * block].astype(F32)).astype(BF16)

    grads_in.wait()
    take = (
        lax.broadcasted_iota(jnp.int32, (lat, seq), 0) + slot
        == lax.broadcasted_iota(jnp.int32, (lat, seq), 1)
    )
    taken = dot(jnp.where(take, 1.0, 0.0).astype(BF16), grads[0]).astype(BF16)

    def upstream(t):
        wo_in[t].wait()
        up = lax.dot_general(
            taken,
            wo[pl.ds(pl.multiple_of(order[t] * block, block), block), :],
            (((1,), (1,)), ((), ())),
            preferred_element_type=F32,
        )
        owner = 1 - core if t < half_groups else core
        u_own[owner, pl.ds((t % half_groups) * HEAD, HEAD), :] = to_cols(up).astype(BF16)

    for t in range(half_groups):
        upstream(t)
    pl.semaphore_wait(barrier, n_dp + n_mp - 2)
    u_pair = pair_copy(u_own.at[1 - core], u_recv, 0)
    u_pair.start()
    for t in range(half_groups, KVH):
        upstream(t)
    u_gather = Gather(chips, chip, core, lambda j, c: u_all.at[j, c], u_send, u_got)
    u_pair.wait()
    u_all[chip, core] = u_own[core] + u_recv[...]
    u_gather.start()

    features_in.wait()
    wide = features[0].astype(F32)
    mean_square = jnp.mean(wide * wide, axis=-1, keepdims=True)
    features[0] = (wide * lax.rsqrt(mean_square + epsilon) * gain[...]).astype(BF16)

    wk_in.wait()
    projected_keys = dot(features[0], wk[...])
    keys_t[...] = projected_keys.T.astype(BF16)
    for g in range(KVH):
        keys[g] = projected_keys[:, g * HEAD : (g + 1) * HEAD].astype(BF16)
    wv_in.wait()
    projected_values = dot(features[0], wv[...])
    values_t[...] = projected_values.T.astype(BF16)
    for g in range(KVH):
        values[g] = projected_values[:, g * HEAD : (g + 1) * HEAD].astype(BF16)

    peaks, totals = ([[], []], [[], []])
    for g in range(KVH):
        scores = dot(keys[g], query_t[g]) * scale
        peak_first = jnp.max(jnp.where(in_first, scores, LOW), axis=0, keepdims=True)
        peak_last = jnp.max(jnp.where(in_first, LOW, scores), axis=0, keepdims=True)
        weight = jnp.exp(scores - jnp.where(in_first, peak_first, peak_last))
        weights[g] = weight
        weight_first = jnp.where(in_first, weight, 0.0)
        weight_last = jnp.where(in_first, 0.0, weight)
        peaks[0].append(peak_first)
        peaks[1].append(peak_last)
        totals[0].append(jnp.sum(weight_first, axis=0, keepdims=True))
        totals[1].append(jnp.sum(weight_last, axis=0, keepdims=True))
        value_cols = values_t[pl.ds(g * HEAD, HEAD), :]
        sums[0, g] = dot(value_cols, weight_first.astype(BF16))
        sums[1, g] = dot(value_cols, weight_last.astype(BF16))

    def to_all(ref, send, recv):
        return Direct(
            chips, chip, core, lambda j, c: ref.at[chip, core], lambda j, c: ref.at[j, c], send, recv
        )

    stats[chip, core] = jnp.concatenate(peaks[0] + totals[0] + peaks[1] + totals[1], axis=0)
    s_gather = to_all(stats, s_send, s_got)
    s_gather.all_start()
    u_gather.forward()
    s_gather.finish()

    own = stats[chip, core]
    parts = []
    for d in range(n_dp):
        got = stats[d // 2, d % 2]
        for part, image in enumerate((image_at(d * tok), image_at(d * tok + tok - 1))):
            at = 2 * KVH * part
            parts.append((image, got[at : at + KVH], got[at + KVH : at + 2 * KVH]))

    def whole(mine, local_peak):
        peak = jnp.full_like(local_peak, LOW)
        for image, part_peak, _ in parts:
            peak = jnp.maximum(peak, jnp.where(image == mine, part_peak, LOW))
        total = jnp.zeros_like(peak)
        for image, part_peak, part_total in parts:
            share = part_total * jnp.exp(part_peak - peak)
            total = total + jnp.where(image == mine, share, 0.0)
        return jnp.exp(local_peak - peak) / total

    factors = (whole(first, own[0:KVH]), whole(last, own[2 * KVH : 3 * KVH]))
    for part in range(2):
        for g in range(KVH):
            rescale[part, g] = factors[part][g : g + 1]
            sums[part, g] = sums[part, g] * factors[part][g : g + 1]
    u_gather.finish()

    chip_first = lax.div(end_first - 1, 2 * tok)
    chip_last = lax.div(end_last - 1, 2 * tok)

    def up_of(where_from, g):
        at = g * HEAD
        return u_all[where_from, at // half, pl.ds(at % half, HEAD), :]

    dots[chip, core] = jnp.concatenate(
        [
            jnp.sum(up_of(where_from, g).astype(F32) * sums[part, g], axis=0, keepdims=True)
            for part, where_from in enumerate((chip_first, chip_last))
            for g in range(KVH)
        ],
        axis=0,
    )
    d_gather = to_all(dots, d_send, d_got)
    d_gather.all_start()
    for g in range(KVH):
        dot_first = dot(values[g], up_of(chip_first, g))
        dot_last = dot(values[g], up_of(chip_last, g))
        chosen[g] = jnp.where(in_first, dot_first, dot_last)
        weights[g] = weights[g] * jnp.where(in_first, rescale[0, g], rescale[1, g])
    d_gather.finish()

    inner_first = jnp.zeros((KVH, dots.shape[3]), F32)
    inner_last = inner_first
    for d in range(n_dp):
        got = dots[d // 2, d % 2]
        for part, image in enumerate((image_at(d * tok), image_at(d * tok + tok - 1))):
            piece = got[part * KVH : (part + 1) * KVH]
            inner_first = inner_first + jnp.where(image == first, piece, 0.0)
            inner_last = inner_last + jnp.where(image == last, piece, 0.0)
    for g in range(KVH):
        rescale[0, g] = inner_first[g : g + 1]
        rescale[1, g] = inner_last[g : g + 1]

    g_rows = g_own.shape[2]
    per_group = chips // KVH
    g_scatter = Direct(
        chips,
        chip,
        core,
        lambda j, c: g_own.at[c, j],
        lambda j, c: g_chip.at[j, c],
        gc_send,
        gc_got,
    )
    my_group = lax.div(chip, per_group)
    for t in (1, 3, 2, 0):
        g = lax.rem(my_group + t, KVH)
        inner = jnp.where(in_first, rescale[0, g], rescale[1, g])
        grad = weights[g] * (chosen[g] - inner)
        cols_t = keys_t[pl.ds(pl.multiple_of(g * HEAD, HEAD), HEAD), :]
        term = (dot(cols_t, grad.astype(BF16)) * scale)
        lanes = term.shape[1] // 2
        for p in range(per_group):
            for c in range(2):
                g_own[c, g * per_group + p] = term[
                    p * g_rows : (p + 1) * g_rows, c * lanes : (c + 1) * lanes
                ].astype(BF16)
        if per_group == 1:
            for q in range(2):
                if t or q:
                    g_scatter.start(t, q)
    if per_group != 1:
        g_scatter.all_start()

    for g in range(KVH):
        share_first = sums[0, g]
        share_last = sums[1, g]
        for i in range(images):
            share = jnp.where(first == i, share_first, 0.0) + jnp.where(last == i, share_last, 0.0)
            at = g * HEAD
            a_own[at // half, pl.ds(i * half + at % half, HEAD), :] = share.astype(BF16)
    a_pair_copy = pair_copy(a_own.at[1 - core], a_recv, 2)
    a_pair_copy.start()

    def scatter(src, rows, dst, send, recv, k, target_chip):
        return pltpu.make_async_remote_copy(
            src_ref=src.at[pl.ds(pl.multiple_of(target_chip * rows, rows), rows)],
            dst_ref=dst.at[k],
            send_sem=send.at[k],
            recv_sem=recv.at[k],
            device_id={"dp": target_chip * 2 + core},
            device_id_type=MESH,
        )

    a_rows = a_pair.shape[0] // chips
    a_pair_copy.wait()
    a_pair[...] = (a_own[core].astype(F32) + a_recv[...].astype(F32)).astype(BF16)
    a_scatter = [
        scatter(a_pair, a_rows, a_chip, ac_send, ac_got, k, lax.rem(chip + k, chips))
        for k in range(1, chips)
    ]
    for copy in a_scatter:
        copy.start()

    g_chip[chip, core] = g_own[core, chip]
    g_scatter.finish()
    g_piece = g_chip[0, 0].astype(F32)
    for d in range(1, n_dp):
        g_piece = g_piece + g_chip[d // 2, d % 2].astype(F32)
    z_all[z] = g_piece
    z_copies = [
        pltpu.make_async_remote_copy(
            src_ref=z_all.at[z],
            dst_ref=z_all.at[z],
            send_sem=z_send.at[k],
            recv_sem=z_got.at[k],
            device_id={"mp": lax.rem(z + k, n_mp)},
            device_id_type=MESH,
        )
        for k in range(1, n_mp)
    ]
    for copy in z_copies:
        copy.start()

    for copy in a_scatter:
        copy.wait()
    a_piece = a_pair[pl.ds(pl.multiple_of(chip * a_rows, a_rows), a_rows), :].astype(F32)
    for k in range(1, chips):
        a_piece = a_piece + a_chip[k].astype(F32)
    a_all[core, pl.ds(pl.multiple_of(chip * a_rows, a_rows), a_rows), :] = a_piece.astype(BF16)
    a_gather = Gather(
        chips,
        chip,
        core,
        lambda j, c: a_all.at[c, pl.ds(pl.multiple_of(j * a_rows, a_rows), a_rows)],
        a_send,
        a_got,
    )
    a_gather.start()

    for k in range(1, n_mp):
        origin = lax.rem(z + n_mp - k, n_mp)
        pltpu.make_async_remote_copy(
            src_ref=z_all.at[origin],
            dst_ref=z_all.at[origin],
            send_sem=z_send.at[k],
            recv_sem=z_got.at[k],
            device_id={"mp": origin},
            device_id_type=MESH,
        ).wait_recv()
    g_sum = z_all[0]
    for k in range(1, n_mp):
        g_sum = g_sum + z_all[k]
    g_all[chip, core] = g_sum.astype(BF16)
    g_gather = to_all(g_all, g_send, g_got)
    g_gather.all_start()
    for copy in z_copies:
        copy.wait_send()

    a_gather.forward()
    a_gather.finish()
    halves = []
    for part in range(2):
        attended = a_all[part, 0:half, :].astype(F32)
        for i in range(1, images):
            other = a_all[part, i * half : (i + 1) * half, :].astype(F32)
            attended = jnp.where(first == i, other, attended)
        halves.append(attended)
    attended_rows = to_rows(jnp.concatenate(halves, axis=0), lat).astype(BF16)
    put = (
        lax.broadcasted_iota(jnp.int32, (seq, lat), 1) + slot
        == lax.broadcasted_iota(jnp.int32, (seq, lat), 0)
    )
    shifted = dot(jnp.where(put, 1.0, 0.0).astype(BF16), attended_rows).astype(BF16)
    row_at = lax.broadcasted_iota(jnp.int32, (seq, 1), 0)
    inside = (row_at >= slot) & (row_at < slot + lat)
    text_in.wait()
    projected = dot(shifted, wo[...]).astype(BF16)
    merged[0] = jnp.where(inside, projected.astype(F32), text[0].astype(F32)).astype(BF16)

    g_gather.finish()
    whole_rows = [
        jnp.concatenate([g_all[j, 0].astype(F32), g_all[j, 1].astype(F32)], axis=1)
        for j in range(chips)
    ]
    query_grad[...] = to_rows(jnp.concatenate(whole_rows, axis=0), lat)


def on_device(
    n_dp, n_mp, features, context_gain, queries, w_key, w_value, w_out, image_tiles, slot_start, text_rows, row_grads
):
    _, tok, width = features.shape
    images = image_tiles.shape[1]
    lat = queries.shape[0]
    _, seq, dm = text_rows.shape
    chips = n_dp // 2
    block = KVH * HEAD
    half = block // 2
    cols = PER * lat
    a_rows = images * half // chips
    g_rows = block // chips
    gathers = pltpu.SemaphoreType.DMA((2 * chips - 1,))
    direct = pltpu.SemaphoreType.DMA((n_dp,))
    vmem = pl.BlockSpec(memory_space=pltpu.VMEM)
    smem = pl.BlockSpec(memory_space=pltpu.SMEM)
    anywhere = pl.BlockSpec(memory_space=pl.ANY)
    return pl.pallas_call(
        functools.partial(kernel, (n_dp, n_mp, images, lat, tok, seq)),
        out_shape=(
            pltpu.VMEM(text_rows.shape, BF16),
            pltpu.VMEM(queries.shape, F32),
        ),
        in_specs=[smem, smem, vmem, vmem] + [anywhere] * 6,
        out_specs=(vmem, vmem),
        scratch_shapes=[
            pltpu.VMEM(features.shape, BF16),
            pltpu.VMEM(w_key.shape, BF16),
            pltpu.VMEM(w_value.shape, BF16),
            pltpu.VMEM(w_out.shape, BF16),
            pltpu.VMEM(text_rows.shape, BF16),
            pltpu.VMEM(row_grads.shape, BF16),
            pltpu.VMEM((KVH, tok, HEAD), BF16),
            pltpu.VMEM((KVH, tok, HEAD), BF16),
            pltpu.VMEM((block, tok), BF16),
            pltpu.VMEM((block, tok), BF16),
            pltpu.VMEM((KVH, HEAD, cols), BF16),
            pltpu.VMEM((KVH, tok, cols), F32),
            pltpu.VMEM((KVH, tok, cols), F32),
            pltpu.VMEM((2, KVH, HEAD, cols), F32),
            pltpu.VMEM((2, half, cols), BF16),
            pltpu.VMEM((half, cols), BF16),
            pltpu.VMEM((chips, 2, half, cols), BF16),
            pltpu.VMEM((chips, 2, 4 * KVH, cols), F32),
            pltpu.VMEM((chips, 2, 2 * KVH, cols), F32),
            pltpu.VMEM((2, KVH, 1, cols), F32),
            pltpu.VMEM((2, chips, g_rows, cols // 2), BF16),
            pltpu.VMEM((chips, 2, g_rows, cols // 2), BF16),
            pltpu.VMEM((n_mp, g_rows, cols // 2), F32),
            pltpu.VMEM((chips, 2, g_rows, cols // 2), BF16),
            pltpu.VMEM((2, images * half, cols), BF16),
            pltpu.VMEM((images * half, cols), BF16),
            pltpu.VMEM((images * half, cols), BF16),
            pltpu.VMEM((chips, a_rows, cols), BF16),
            pltpu.VMEM((2, images * half, cols), BF16),
            pltpu.SemaphoreType.DMA((5 + KVH,)),
            pltpu.SemaphoreType.DMA((3,)),
            pltpu.SemaphoreType.DMA((3,)),
            gathers,
            gathers,
            direct,
            direct,
            direct,
            direct,
            direct,
            direct,
            pltpu.SemaphoreType.DMA((n_mp,)),
            pltpu.SemaphoreType.DMA((n_mp,)),
            direct,
            direct,
            pltpu.SemaphoreType.DMA((chips,)),
            pltpu.SemaphoreType.DMA((chips,)),
            gathers,
            gathers,
        ],
        compiler_params=pltpu.CompilerParams(
            collective_id=0, has_side_effects=True, vmem_limit_bytes=60 * 1024 * 1024
        ),
        name="resampler",
    )(
        image_tiles,
        slot_start,
        context_gain,
        queries,
        features,
        w_key,
        w_value,
        w_out,
        text_rows,
        row_grads,
    )


def solution(mesh):
    placed = (
        P("mp", "dp", None),
        P(),
        P(),
        P(),
        P(),
        P(),
        P("mp", None),
        P("mp", None),
        P("mp", "dp", None),
        P("mp", "dp", None),
    )
    return jax.shard_map(
        functools.partial(on_device, mesh.shape["dp"], mesh.shape["mp"]),
        mesh=mesh,
        in_specs=placed,
        out_specs=(P("mp", "dp", None), P()),
        check_vma=False,
    )
```

```python
import functools

import jax
import jax.numpy as jnp
from jax import lax
from jax.experimental import pallas as pl
from jax.experimental.pallas import tpu as pltpu
from jax.sharding import PartitionSpec as P

HEADS = 16
HEAD = 96
KVH = 4
PER = HEADS // KVH
epsilon = 1e-06
LOW = -1e30
MESH = pl.DeviceIdType.MESH
F32 = jnp.float32
BF16 = jnp.bfloat16


def to_cols(rows):
    stacked = jnp.concatenate([rows[:, c * HEAD : (c + 1) * HEAD] for c in range(PER)], axis=0)
    return stacked.T


def to_rows(cols, lat):
    flipped = cols.T
    return jnp.concatenate(
        [
            flipped[c * lat : (c + 1) * lat, g * HEAD : (g + 1) * HEAD]
            for g in range(KVH)
            for c in range(PER)
        ],
        axis=1,
    )


def dot(a, b):
    return jnp.dot(a, b, preferred_element_type=F32)


class Gather:
    def __init__(self, chips, chip, core, at, send, recv):
        self.chips, self.chip, self.core = chips, chip, core
        self.at, self.send, self.recv = at, send, recv

    def hop(self, slot_chip, sem, target):
        ref = self.at(slot_chip, self.core)
        return pltpu.make_async_remote_copy(
            src_ref=ref,
            dst_ref=ref,
            send_sem=self.send.at[sem],
            recv_sem=self.recv.at[sem],
            device_id={"dp": target},
            device_id_type=MESH,
        )

    def start(self):
        for k in range(1, self.chips):
            there = lax.rem(self.chip + k, self.chips)
            self.hop(self.chip, k, there * 2 + self.core).start()
        self.hop(self.chip, 0, self.chip * 2 + 1 - self.core).start()

    def forward(self):
        for k in range(1, self.chips):
            origin = lax.rem(self.chip + self.chips - k, self.chips)
            self.hop(origin, k, origin * 2 + self.core).wait_recv()
            self.hop(origin, self.chips - 1 + k, self.chip * 2 + 1 - self.core).start()

    def finish(self):
        mate = self.chip * 2 + 1 - self.core
        for k in range(self.chips):
            origin = lax.rem(self.chip + self.chips - k, self.chips)
            ref = self.at(origin, 1 - self.core)
            sem = 0 if k == 0 else self.chips - 1 + k
            pltpu.make_async_remote_copy(
                src_ref=ref,
                dst_ref=ref,
                send_sem=self.send.at[sem],
                recv_sem=self.recv.at[sem],
                device_id={"dp": mate},
                device_id_type=MESH,
            ).wait_recv()
        for sem in range(2 * self.chips - 1):
            self.hop(self.chip, sem, mate).wait_send()


class Direct:
    def __init__(self, chips, chip, core, src, dst, send, recv):
        self.chips, self.chip, self.core = chips, chip, core
        self.src, self.dst, self.send, self.recv = src, dst, send, recv

    def hop(self, k, q, origin, target):
        return pltpu.make_async_remote_copy(
            src_ref=self.src(*target),
            dst_ref=self.dst(*origin),
            send_sem=self.send.at[2 * k + q],
            recv_sem=self.recv.at[2 * k + q],
            device_id={"dp": target[0] * 2 + target[1]},
            device_id_type=MESH,
        )

    def other(self, k, q):
        return (lax.rem(self.chip + k, self.chips), 1 - self.core if q else self.core)

    def start(self, k, q):
        self.hop(k, q, (self.chip, self.core), self.other(k, q)).start()

    def all_start(self):
        for k in list(range(1, self.chips)) + [0]:
            for q in range(2):
                if k or q:
                    self.start(k, q)

    def finish(self):
        for k in range(self.chips):
            for q in range(2):
                if k or q:
                    origin = self.other(self.chips - k, q)
                    self.hop(k, q, origin, origin).wait_recv()
        for k in range(self.chips):
            for q in range(2):
                if k or q:
                    self.hop(k, q, (self.chip, self.core), self.other(k, q)).wait_send()


def kernel(
    dims,
    tiles,
    slots,
    gain,
    queries,
    features_hbm,
    wk_hbm,
    wv_hbm,
    wo_hbm,
    text_hbm,
    grads_hbm,
    merged,
    query_grad,
    features,
    wk,
    wv,
    wo,
    text,
    grads,
    keys,
    values,
    keys_t,
    values_t,
    query_t,
    weights,
    chosen,
    sums,
    t_own,
    t_recv,
    u_all,
    stats,
    dots,
    rescale,
    g_own,
    g_chip,
    z_all,
    g_all,
    a_own,
    a_recv,
    a_pair,
    a_chip,
    a_all,
    load_sem,
    pair_send,
    pair_recv,
    u_send,
    u_got,
    s_send,
    s_got,
    d_send,
    d_got,
    gc_send,
    gc_got,
    z_send,
    z_got,
    g_send,
    g_got,
    ac_send,
    ac_got,
    a_send,
    a_got,
):
    n_dp, n_mp, images, lat, tok, seq = dims
    chips = n_dp // 2
    me = lax.axis_index("dp")
    z = lax.axis_index("mp")
    chip = lax.div(me, 2)
    core = lax.rem(me, 2)
    mate = chip * 2 + 1 - core
    scale = HEAD ** (-0.5)
    half = KVH * HEAD // 2
    block = KVH * HEAD

    loads = []

    def load(src, dst, at):
        copy = pltpu.make_async_copy(src, dst, load_sem.at[at])
        copy.start()
        return copy

    def load_out(at, g):
        part = pl.ds(pl.multiple_of(g * block, block), block)
        return load(wo_hbm.at[part], wo.at[part], 2 + at)

    half_groups = KVH // 2
    order = [core * half_groups + t for t in range(half_groups)]
    order += [(1 - core) * half_groups + t for t in range(half_groups)]
    grads_in = load(grads_hbm, grads, 1)
    features_in = load(features_hbm, features, 0)
    wk_in = load(wk_hbm, wk, 2 + KVH)
    wo_in = [load_out(t, order[t]) for t in range(half_groups)]
    wv_in = load(wv_hbm, wv, 3 + KVH)
    text_in = load(text_hbm, text, 4 + KVH)
    wo_in += [load_out(t, order[t]) for t in range(half_groups, KVH)]

    barrier = pltpu.get_barrier_semaphore()
    for k in range(1, n_dp):
        pl.semaphore_signal(
            barrier, inc=1, device_id={"dp": lax.rem(me + k, n_dp)}, device_id_type=MESH
        )
    for k in range(1, n_mp):
        pl.semaphore_signal(
            barrier, inc=1, device_id={"mp": lax.rem(z + k, n_mp)}, device_id_type=MESH
        )

    def pair_copy(src, dst, at):
        return pltpu.make_async_remote_copy(
            src_ref=src,
            dst_ref=dst,
            send_sem=pair_send.at[at],
            recv_sem=pair_recv.at[at],
            device_id={"dp": mate},
            device_id_type=MESH,
        )

    first_row = me * tok
    ends = []
    running = jnp.int32(0)
    for i in range(images):
        running = running + tiles[0, i]
        ends.append(running)

    def image_at(row):
        found = jnp.int32(0)
        for end in ends:
            found = found + jnp.where(row >= end, 1, 0)
        return found

    def pick(options, index):
        chosen_one = options[0]
        for i in range(1, images):
            chosen_one = jnp.where(index == i, options[i], chosen_one)
        return chosen_one

    first = image_at(first_row)
    last = image_at(first_row + tok - 1)
    end_first = pick(ends, first)
    end_last = pick(ends, last)
    ends_here = end_first <= first_row + tok
    slot = pick([slots[0, i] for i in range(images)], first)
    slot = jnp.where(ends_here, slot, 2 * seq)
    rows_at = first_row + lax.broadcasted_iota(jnp.int32, (tok, 1), 0)
    in_first = rows_at < end_first

    for g in range(KVH):
        query_t[g] = to_cols(queries[:, g * block : (g + 1) * block].astype(F32)).astype(BF16)

    grads_in.wait()
    take = (
        lax.broadcasted_iota(jnp.int32, (lat, seq), 0) + slot
        == lax.broadcasted_iota(jnp.int32, (lat, seq), 1)
    )
    t_own[...] = dot(jnp.where(take, 1.0, 0.0).astype(BF16), grads[0]).astype(BF16)
    pl.semaphore_wait(barrier, n_dp + n_mp - 2)
    t_pair = pair_copy(t_own, t_recv, 0)
    t_pair.start()

    features_in.wait()
    wide = features[0].astype(F32)
    mean_square = jnp.mean(wide * wide, axis=-1, keepdims=True)
    features[0] = (wide * lax.rsqrt(mean_square + epsilon) * gain[...]).astype(BF16)

    wk_in.wait()
    projected_keys = dot(features[0], wk[...])
    keys_t[...] = projected_keys.T.astype(BF16)
    for g in range(KVH):
        keys[g] = projected_keys[:, g * HEAD : (g + 1) * HEAD].astype(BF16)
    t_pair.wait()
    taken = t_own[...] + t_recv[...]
    for t in range(half_groups):
        wo_in[t].wait()
        up = lax.dot_general(
            taken,
            wo[pl.ds(pl.multiple_of(order[t] * block, block), block), :],
            (((1,), (1,)), ((), ())),
            preferred_element_type=F32,
        )
        u_all[chip, core, pl.ds(t * HEAD, HEAD), :] = to_cols(up).astype(BF16)
    u_gather = Gather(chips, chip, core, lambda j, c: u_all.at[j, c], u_send, u_got)
    u_gather.start()
    wv_in.wait()
    projected_values = dot(features[0], wv[...])
    values_t[...] = projected_values.T.astype(BF16)
    for g in range(KVH):
        values[g] = projected_values[:, g * HEAD : (g + 1) * HEAD].astype(BF16)

    peaks, totals = ([[], []], [[], []])
    for g in range(KVH):
        scores = dot(keys[g], query_t[g]) * scale
        peak_first = jnp.max(jnp.where(in_first, scores, LOW), axis=0, keepdims=True)
        peak_last = jnp.max(jnp.where(in_first, LOW, scores), axis=0, keepdims=True)
        weight = jnp.exp(scores - jnp.where(in_first, peak_first, peak_last))
        weights[g] = weight
        weight_first = jnp.where(in_first, weight, 0.0)
        weight_last = jnp.where(in_first, 0.0, weight)
        peaks[0].append(peak_first)
        peaks[1].append(peak_last)
        totals[0].append(jnp.sum(weight_first, axis=0, keepdims=True))
        totals[1].append(jnp.sum(weight_last, axis=0, keepdims=True))
        value_cols = values_t[pl.ds(g * HEAD, HEAD), :]
        sums[0, g] = dot(value_cols, weight_first.astype(BF16))
        sums[1, g] = dot(value_cols, weight_last.astype(BF16))

    def to_all(ref, send, recv):
        return Direct(
            chips, chip, core, lambda j, c: ref.at[chip, core], lambda j, c: ref.at[j, c], send, recv
        )

    stats[chip, core] = jnp.concatenate(peaks[0] + totals[0] + peaks[1] + totals[1], axis=0)
    s_gather = to_all(stats, s_send, s_got)
    s_gather.all_start()
    u_gather.forward()
    s_gather.finish()

    own = stats[chip, core]
    parts = []
    for d in range(n_dp):
        got = stats[d // 2, d % 2]
        for part, image in enumerate((image_at(d * tok), image_at(d * tok + tok - 1))):
            at = 2 * KVH * part
            parts.append((image, got[at : at + KVH], got[at + KVH : at + 2 * KVH]))

    def whole(mine, local_peak):
        peak = jnp.full_like(local_peak, LOW)
        for image, part_peak, _ in parts:
            peak = jnp.maximum(peak, jnp.where(image == mine, part_peak, LOW))
        total = jnp.zeros_like(peak)
        for image, part_peak, part_total in parts:
            share = part_total * jnp.exp(part_peak - peak)
            total = total + jnp.where(image == mine, share, 0.0)
        return jnp.exp(local_peak - peak) / total

    factors = (whole(first, own[0:KVH]), whole(last, own[2 * KVH : 3 * KVH]))
    for part in range(2):
        for g in range(KVH):
            rescale[part, g] = factors[part][g : g + 1]
            sums[part, g] = sums[part, g] * factors[part][g : g + 1]
    u_gather.finish()

    chip_first = lax.div(end_first - 1, 2 * tok)
    chip_last = lax.div(end_last - 1, 2 * tok)

    def up_of(where_from, g):
        at = g * HEAD
        return u_all[where_from, at // half, pl.ds(at % half, HEAD), :]

    dots[chip, core] = jnp.concatenate(
        [
            jnp.sum(up_of(where_from, g).astype(F32) * sums[part, g], axis=0, keepdims=True)
            for part, where_from in enumerate((chip_first, chip_last))
            for g in range(KVH)
        ],
        axis=0,
    )
    d_gather = to_all(dots, d_send, d_got)
    d_gather.all_start()
    for g in range(KVH):
        dot_first = dot(values[g], up_of(chip_first, g))
        dot_last = dot(values[g], up_of(chip_last, g))
        chosen[g] = jnp.where(in_first, dot_first, dot_last)
        weights[g] = weights[g] * jnp.where(in_first, rescale[0, g], rescale[1, g])
    d_gather.finish()

    inner_first = jnp.zeros((KVH, dots.shape[3]), F32)
    inner_last = inner_first
    for d in range(n_dp):
        got = dots[d // 2, d % 2]
        for part, image in enumerate((image_at(d * tok), image_at(d * tok + tok - 1))):
            piece = got[part * KVH : (part + 1) * KVH]
            inner_first = inner_first + jnp.where(image == first, piece, 0.0)
            inner_last = inner_last + jnp.where(image == last, piece, 0.0)
    for g in range(KVH):
        rescale[0, g] = inner_first[g : g + 1]
        rescale[1, g] = inner_last[g : g + 1]

    g_rows = g_own.shape[2]
    per_group = chips // KVH
    g_scatter = Direct(
        chips,
        chip,
        core,
        lambda j, c: g_own.at[c, j],
        lambda j, c: g_chip.at[j, c],
        gc_send,
        gc_got,
    )
    my_group = lax.div(chip, per_group)
    for t in (1, 3, 2, 0):
        g = lax.rem(my_group + t, KVH)
        inner = jnp.where(in_first, rescale[0, g], rescale[1, g])
        grad = weights[g] * (chosen[g] - inner)
        cols_t = keys_t[pl.ds(pl.multiple_of(g * HEAD, HEAD), HEAD), :]
        term = (dot(cols_t, grad.astype(BF16)) * scale)
        lanes = term.shape[1] // 2
        for p in range(per_group):
            for c in range(2):
                g_own[c, g * per_group + p] = term[
                    p * g_rows : (p + 1) * g_rows, c * lanes : (c + 1) * lanes
                ].astype(BF16)
        if per_group == 1:
            for q in range(2):
                if t or q:
                    g_scatter.start(t, q)
    if per_group != 1:
        g_scatter.all_start()

    for g in range(KVH):
        share_first = sums[0, g]
        share_last = sums[1, g]
        for i in range(images):
            share = jnp.where(first == i, share_first, 0.0) + jnp.where(last == i, share_last, 0.0)
            at = g * HEAD
            a_own[at // half, pl.ds(i * half + at % half, HEAD), :] = share.astype(BF16)
    a_pair_copy = pair_copy(a_own.at[1 - core], a_recv, 2)
    a_pair_copy.start()

    def scatter(src, rows, dst, send, recv, k, target_chip):
        return pltpu.make_async_remote_copy(
            src_ref=src.at[pl.ds(pl.multiple_of(target_chip * rows, rows), rows)],
            dst_ref=dst.at[k],
            send_sem=send.at[k],
            recv_sem=recv.at[k],
            device_id={"dp": target_chip * 2 + core},
            device_id_type=MESH,
        )

    a_rows = a_pair.shape[0] // chips
    a_pair_copy.wait()
    a_pair[...] = (a_own[core].astype(F32) + a_recv[...].astype(F32)).astype(BF16)
    a_scatter = [
        scatter(a_pair, a_rows, a_chip, ac_send, ac_got, k, lax.rem(chip + k, chips))
        for k in range(1, chips)
    ]
    for copy in a_scatter:
        copy.start()

    g_chip[chip, core] = g_own[core, chip]
    g_scatter.finish()
    g_piece = g_chip[0, 0].astype(F32)
    for d in range(1, n_dp):
        g_piece = g_piece + g_chip[d // 2, d % 2].astype(F32)
    z_all[z] = g_piece
    z_copies = [
        pltpu.make_async_remote_copy(
            src_ref=z_all.at[z],
            dst_ref=z_all.at[z],
            send_sem=z_send.at[k],
            recv_sem=z_got.at[k],
            device_id={"mp": lax.rem(z + k, n_mp)},
            device_id_type=MESH,
        )
        for k in range(1, n_mp)
    ]
    for copy in z_copies:
        copy.start()

    for copy in a_scatter:
        copy.wait()
    a_piece = a_pair[pl.ds(pl.multiple_of(chip * a_rows, a_rows), a_rows), :].astype(F32)
    for k in range(1, chips):
        a_piece = a_piece + a_chip[k].astype(F32)
    a_all[core, pl.ds(pl.multiple_of(chip * a_rows, a_rows), a_rows), :] = a_piece.astype(BF16)
    a_gather = Gather(
        chips,
        chip,
        core,
        lambda j, c: a_all.at[c, pl.ds(pl.multiple_of(j * a_rows, a_rows), a_rows)],
        a_send,
        a_got,
    )
    a_gather.start()

    for k in range(1, n_mp):
        origin = lax.rem(z + n_mp - k, n_mp)
        pltpu.make_async_remote_copy(
            src_ref=z_all.at[origin],
            dst_ref=z_all.at[origin],
            send_sem=z_send.at[k],
            recv_sem=z_got.at[k],
            device_id={"mp": origin},
            device_id_type=MESH,
        ).wait_recv()
    g_sum = z_all[0]
    for k in range(1, n_mp):
        g_sum = g_sum + z_all[k]
    g_all[chip, core] = g_sum.astype(BF16)
    g_gather = to_all(g_all, g_send, g_got)
    g_gather.all_start()
    for copy in z_copies:
        copy.wait_send()

    a_gather.forward()
    a_gather.finish()
    halves = []
    for part in range(2):
        attended = a_all[part, 0:half, :].astype(F32)
        for i in range(1, images):
            other = a_all[part, i * half : (i + 1) * half, :].astype(F32)
            attended = jnp.where(first == i, other, attended)
        halves.append(attended)
    attended_rows = to_rows(jnp.concatenate(halves, axis=0), lat).astype(BF16)
    put = (
        lax.broadcasted_iota(jnp.int32, (seq, lat), 1) + slot
        == lax.broadcasted_iota(jnp.int32, (seq, lat), 0)
    )
    shifted = dot(jnp.where(put, 1.0, 0.0).astype(BF16), attended_rows).astype(BF16)
    row_at = lax.broadcasted_iota(jnp.int32, (seq, 1), 0)
    inside = (row_at >= slot) & (row_at < slot + lat)
    text_in.wait()
    for t in range(half_groups, KVH):
        wo_in[t].wait()
    projected = dot(shifted, wo[...]).astype(BF16)
    merged[0] = jnp.where(inside, projected.astype(F32), text[0].astype(F32)).astype(BF16)

    g_gather.finish()
    whole_rows = [
        jnp.concatenate([g_all[j, 0].astype(F32), g_all[j, 1].astype(F32)], axis=1)
        for j in range(chips)
    ]
    query_grad[...] = to_rows(jnp.concatenate(whole_rows, axis=0), lat)


def on_device(
    n_dp, n_mp, features, context_gain, queries, w_key, w_value, w_out, image_tiles, slot_start, text_rows, row_grads
):
    _, tok, width = features.shape
    images = image_tiles.shape[1]
    lat = queries.shape[0]
    _, seq, dm = text_rows.shape
    chips = n_dp // 2
    block = KVH * HEAD
    half = block // 2
    cols = PER * lat
    a_rows = images * half // chips
    g_rows = block // chips
    gathers = pltpu.SemaphoreType.DMA((2 * chips - 1,))
    direct = pltpu.SemaphoreType.DMA((n_dp,))
    vmem = pl.BlockSpec(memory_space=pltpu.VMEM)
    smem = pl.BlockSpec(memory_space=pltpu.SMEM)
    anywhere = pl.BlockSpec(memory_space=pl.ANY)
    return pl.pallas_call(
        functools.partial(kernel, (n_dp, n_mp, images, lat, tok, seq)),
        out_shape=(
            pltpu.VMEM(text_rows.shape, BF16),
            pltpu.VMEM(queries.shape, F32),
        ),
        in_specs=[smem, smem, vmem, vmem] + [anywhere] * 6,
        out_specs=(vmem, vmem),
        scratch_shapes=[
            pltpu.VMEM(features.shape, BF16),
            pltpu.VMEM(w_key.shape, BF16),
            pltpu.VMEM(w_value.shape, BF16),
            pltpu.VMEM(w_out.shape, BF16),
            pltpu.VMEM(text_rows.shape, BF16),
            pltpu.VMEM(row_grads.shape, BF16),
            pltpu.VMEM((KVH, tok, HEAD), BF16),
            pltpu.VMEM((KVH, tok, HEAD), BF16),
            pltpu.VMEM((block, tok), BF16),
            pltpu.VMEM((block, tok), BF16),
            pltpu.VMEM((KVH, HEAD, cols), BF16),
            pltpu.VMEM((KVH, tok, cols), F32),
            pltpu.VMEM((KVH, tok, cols), F32),
            pltpu.VMEM((2, KVH, HEAD, cols), F32),
            pltpu.VMEM((lat, dm), BF16),
            pltpu.VMEM((lat, dm), BF16),
            pltpu.VMEM((chips, 2, half, cols), BF16),
            pltpu.VMEM((chips, 2, 4 * KVH, cols), F32),
            pltpu.VMEM((chips, 2, 2 * KVH, cols), F32),
            pltpu.VMEM((2, KVH, 1, cols), F32),
            pltpu.VMEM((2, chips, g_rows, cols // 2), BF16),
            pltpu.VMEM((chips, 2, g_rows, cols // 2), BF16),
            pltpu.VMEM((n_mp, g_rows, cols // 2), F32),
            pltpu.VMEM((chips, 2, g_rows, cols // 2), BF16),
            pltpu.VMEM((2, images * half, cols), BF16),
            pltpu.VMEM((images * half, cols), BF16),
            pltpu.VMEM((images * half, cols), BF16),
            pltpu.VMEM((chips, a_rows, cols), BF16),
            pltpu.VMEM((2, images * half, cols), BF16),
            pltpu.SemaphoreType.DMA((5 + KVH,)),
            pltpu.SemaphoreType.DMA((3,)),
            pltpu.SemaphoreType.DMA((3,)),
            gathers,
            gathers,
            direct,
            direct,
            direct,
            direct,
            direct,
            direct,
            pltpu.SemaphoreType.DMA((n_mp,)),
            pltpu.SemaphoreType.DMA((n_mp,)),
            direct,
            direct,
            pltpu.SemaphoreType.DMA((chips,)),
            pltpu.SemaphoreType.DMA((chips,)),
            gathers,
            gathers,
        ],
        compiler_params=pltpu.CompilerParams(
            collective_id=0, has_side_effects=True, vmem_limit_bytes=60 * 1024 * 1024
        ),
        name="resampler",
    )(
        image_tiles,
        slot_start,
        context_gain,
        queries,
        features,
        w_key,
        w_value,
        w_out,
        text_rows,
        row_grads,
    )


def solution(mesh):
    placed = (
        P("mp", "dp", None),
        P(),
        P(),
        P(),
        P(),
        P(),
        P("mp", None),
        P("mp", None),
        P("mp", "dp", None),
        P("mp", "dp", None),
    )
    return jax.shard_map(
        functools.partial(on_device, mesh.shape["dp"], mesh.shape["mp"]),
        mesh=mesh,
        in_specs=placed,
        out_specs=(P("mp", "dp", None), P()),
        check_vma=False,
    )
```
